32 devices in a mesh: dp: 8 (over z, y), tensor: 4 (over x, core).
Axes of the slice: x: 2, y: 2, z: 4, core: 2. Of those that a mesh axis runs over, the one named last changes fastest.
Arguments:
- tokens: bfloat16 [8192, 1024], P(('dp', 'tensor')), may hold values from -6 to 6
- teacher: bfloat16 [8192, 1024], P(('dp', 'tensor')), may hold values from -6 to 6
- cotangent: bfloat16 [8192, 1024], P(('dp', 'tensor')), may hold values from -6 to 6
- loss_mask: int32 [8192], P(('dp', 'tensor')), may hold values from 0 to 1, as said below
- gain_attn: float32 [1024], P(('dp', 'tensor')), may hold values from 0.5 to 1.5
- attn_in: bfloat16 [1024, 3, 1024], P('dp', None, 'tensor'), may hold values from -0.1875 to 0.1875
- attn_out: bfloat16 [1024, 1024], P('tensor', 'dp'), may hold values from -1.5 to 1.5
- gain_ffn: float32 [1024], P(('dp', 'tensor')), may hold values from 0.5 to 1.5
- ffn_in: bfloat16 [1024, 2, 2816], P('dp', None, 'tensor'), may hold values from -0.1875 to 0.1875
- ffn_out: bfloat16 [2816, 1024], P('tensor', 'dp'), may hold values from -0.109375 to 0.109375
Outputs:
- output: bfloat16 [8192, 1024], P(('dp', 'tensor'))
- loss: float32 [], replicated
- grad_tokens: float32 [8192, 1024], P(('dp', 'tensor'))
- grad_gain_attn: float32 [1024], P(('dp', 'tensor'))
- grad_attn_in: float32 [1024, 3, 1024], P('dp', None, 'tensor')
- grad_attn_out: float32 [1024, 1024], P('tensor', 'dp')
- grad_gain_ffn: float32 [1024], P(('dp', 'tensor'))
- grad_ffn_in: float32 [1024, 2, 2816], P('dp', None, 'tensor')
- grad_ffn_out: float32 [2816, 1024], P('tensor', 'dp')
The draws below stay inside these ranges and needn't reach their ends.
Inputs may be any that keep to these rules, and one draw needn't show every extreme that they name: `loss_mask`: 1 flags a patch for the teacher loss; in each aligned block of 256 patches the last one is flagged.
All inputs are finite; a program needn't handle non-finite values.
Results may differ from the reference program's by a relative error of at most 0.014.
Values may be sent and summed in bfloat16 or wider, within the bound.
No kernel may reach another device: no remote copies, remote signals or barrier semaphores. Data moves between devices by JAX's collectives and lax.ppermute only.
A program may use at most 128 MiB of HBM per device.

```python
import jax
import jax.numpy as jnp
from jax import lax

D = 1024
H = 16
HD = 64
FF = 2816
BLOCK = 256
TOK_DEV = 256
SEQ_LEN = 1024
TOKENS = 8192
N_DP = 8


def draw_loss_mask(key, part):
    position = jnp.arange(TOKENS, dtype=jnp.int32)
    chance_level = 250 + 500 * position // TOKENS
    ticket = jax.random.randint(key, (TOKENS,), 0, 1000, dtype=jnp.int32)
    flagged = (ticket < chance_level).astype(jnp.int32)
    closing = position % TOK_DEV == TOK_DEV - 1
    return jnp.where(closing, 1, flagged).astype(jnp.int32)


def block_levels(own_key, shape, split, smallest, high):
    factor_of = 1.0
    for dim, parts in split:
        draws = jax.random.uniform(jax.random.fold_in(jax.random.fold_in(own_key, 6), dim), (parts,), jnp.float32, smallest / len(split), high / len(split))
        factor_of = factor_of * jnp.repeat(jnp.exp(draws), shape[dim] // parts).reshape((-1,) + (1,) * (len(shape) - 1 - dim))
    return factor_of


def gaussian(key, shape, deviation, bound, cuts=(), kind=jnp.bfloat16):
    entries = deviation * jax.random.normal(key, shape, jnp.float32)
    if cuts:
        entries = entries * block_levels(key, shape, cuts, -0.22, 0.18)
    return jnp.clip(entries, -bound, bound).astype(kind)


def setup_inputs(seed: int = 0) -> dict:
    key_list = jax.random.split(jax.random.key(seed), 11)
    tokens = gaussian(key_list[0], (TOKENS, D), 1.0, 6.0, ((0, 32),))
    teacher = gaussian(key_list[1], (TOKENS, D), 1.0, 6.0, ((0, 32),))
    cotangent = gaussian(key_list[2], (TOKENS, D), 1.0, 6.0, ((0, 32),))
    loss_mask = draw_loss_mask(jax.random.fold_in(key_list[10], 71), 0)
    gain_attn = jnp.clip(1.0 + 0.1 * jax.random.normal(key_list[4], (D,), jnp.float32), 0.5, 1.5)
    attn_in = gaussian(key_list[5], (D, 3, D), D ** -0.5, 0.1875, ((0, 8), (2, 4)))
    attn_out = gaussian(key_list[6], (D, D), (D // 64) ** -0.5, 1.5, ((0, 4), (1, 8)))
    gain_ffn = jnp.clip(1.0 + 0.1 * jax.random.normal(key_list[7], (D,), jnp.float32), 0.5, 1.5)
    ffn_in = gaussian(key_list[8], (D, 2, FF), D ** -0.5, 0.1875, ((0, 8), (2, 4)))
    ffn_out = gaussian(key_list[9], (FF, D), FF ** -0.5, 0.109375, ((0, 4), (1, 8)))
    return {"tokens": tokens, "teacher": teacher, "cotangent": cotangent, "loss_mask": loss_mask, "gain_attn": gain_attn, "attn_in": attn_in, "attn_out": attn_out, "gain_ffn": gain_ffn, "ffn_in": ffn_in, "ffn_out": ffn_out}


EPSILON = 1e-05
NEGATIVE = -1e+30
SCORE_SCALE = 0.125

@jax.custom_vjp
def low(v):
    return lax.optimization_barrier(v.astype(jnp.bfloat16)).astype(jnp.float32)

@jax.custom_vjp
def low_back(v):
    return v

def low_keep(v):
    return (low(v), None)

def low_pass(kept, grad):
    return (grad,)

def back_keep(v):
    return (v, None)

def back_low(kept, grad):
    return (low(grad),)
low.defvjp(low_keep, low_pass)
low_back.defvjp(back_keep, back_low)

def rounded(values):
    return low(low_back(values))

def norm_rows(values, gain):
    inverse = lax.rsqrt(lax.optimization_barrier(jnp.mean(values * values, axis=-1, keepdims=True)) + EPSILON)
    return values * inverse * gain

def attend_block(query_block, key_rows, value_rows, row_start):
    raw_scores = jnp.einsum('qhd,khd->hqk', query_block, key_rows, precision=lax.Precision.HIGHEST)
    scores = low_back(raw_scores) * SCORE_SCALE
    query_ids = row_start + jnp.arange(query_block.shape[0]).astype(jnp.int32)
    key_ids = jnp.arange(key_rows.shape[0]).astype(jnp.int32)
    allowed = key_ids[None, :] // BLOCK <= query_ids[:, None] // BLOCK
    scores = jnp.where(allowed[None], scores, NEGATIVE)
    maxima = lax.optimization_barrier(jnp.max(scores, axis=-1, keepdims=True))
    exponent = jnp.exp(scores - maxima)
    shares = exponent / lax.optimization_barrier(jnp.sum(exponent, axis=-1, keepdims=True))
    return jnp.einsum('hqk,khd->qhd', low(shares), value_rows, precision=lax.Precision.HIGHEST)

def layer(inputs, gain_attn, attn_in, attn_out, gain_ffn, ffn_in, ffn_out):
    length = inputs.shape[0]
    normed_a = low(norm_rows(inputs, gain_attn))
    projected = rounded(jnp.einsum('td,dch->tch', normed_a, attn_in, precision=lax.Precision.HIGHEST))
    queries = projected[:, 0].reshape(length, H, HD)
    key_rows = projected[:, 1].reshape(length, H, HD)
    value_rows = projected[:, 2].reshape(length, H, HD)
    block_rows = min(512, length)
    query_blocks = queries.reshape(length // block_rows, block_rows, H, HD)
    block_starts = (jnp.arange(length // block_rows) * block_rows).astype(jnp.int32)
    checked = jax.checkpoint(attend_block)
    mixed = lax.map(lambda pair_item: checked(pair_item[0], key_rows, value_rows, pair_item[1]), (query_blocks, block_starts))
    mixed = rounded(mixed.reshape(length, H * HD))
    hidden_in = inputs + low_back(jnp.dot(mixed, attn_out, precision=lax.Precision.HIGHEST))
    normed_f = low(norm_rows(hidden_in, gain_ffn))
    gate_up = low_back(jnp.einsum('td,dch->tch', normed_f, ffn_in, precision=lax.Precision.HIGHEST))
    inner = low(jax.nn.silu(gate_up[:, 0]) * gate_up[:, 1])
    return hidden_in + low_back(jnp.dot(inner, ffn_out, precision=lax.Precision.HIGHEST))

def reference(tokens, teacher, cotangent, loss_mask, gain_attn, attn_in, attn_out, gain_ffn, ffn_in, ffn_out):
    params = (gain_attn.astype(jnp.float32), attn_in.astype(jnp.float32), attn_out.astype(jnp.float32), gain_ffn.astype(jnp.float32), ffn_in.astype(jnp.float32), ffn_out.astype(jnp.float32))
    flagged = loss_mask.astype(jnp.float32)
    count_all = jnp.sum(flagged)
    loss_weight = TOKENS / count_all
    stacked = (tokens.astype(jnp.float32).reshape(N_DP, SEQ_LEN, D), teacher.astype(jnp.float32).reshape(N_DP, SEQ_LEN, D), cotangent.astype(jnp.float32).reshape(N_DP, SEQ_LEN, D), flagged.reshape(N_DP, SEQ_LEN))

    def one_sequence(carry, seq_item):
        seq_rows, seq_teacher, seq_cot, seq_flags = seq_item

        def objective(weights, row_values):
            result = layer(row_values, weights[0], weights[1], weights[2], weights[3], weights[4], weights[5])
            differ = result - seq_teacher
            error = jnp.sum(seq_flags[:, None] * differ * differ)
            return (jnp.sum(seq_cot * result) + loss_weight * error, (result, error))
        objective_value, pullback, aux_parts = jax.vjp(objective, params, seq_rows, has_aux=True)
        grad_parts, grad_rows = pullback(jnp.ones_like(objective_value))
        total_grads, total_error = carry
        total_grads = jax.tree.map(jnp.add, total_grads, grad_parts)
        return ((total_grads, total_error + aux_parts[1]), (aux_parts[0].astype(jnp.bfloat16), grad_rows))
    start_carry = (jax.tree.map(jnp.zeros_like, params), jnp.zeros((), jnp.float32))
    (grad_parts, error_sum), (outputs, grad_rows) = lax.scan(one_sequence, start_carry, stacked)
    loss = error_sum / (count_all * D)
    return (outputs.reshape(TOKENS, D), loss, grad_rows.reshape(TOKENS, D), grad_parts[0], grad_parts[1], grad_parts[2], grad_parts[3], grad_parts[4], grad_parts[5])
```

```python
import jax
import jax.numpy as jnp
from jax import lax
from jax.experimental import pallas as pl
from jax.experimental.pallas import tpu as pltpu
from jax.sharding import PartitionSpec as P

HD = 64
BLOCK = 256
EPSILON = 1e-05
SCORE_SCALE = 0.125
LOG2E = 1.4426950408889634
BF = jnp.bfloat16
F32 = jnp.float32

RING = (0, 2, 4, 6, 7, 5, 3, 1)
OFFS = (0, -1, 1, -2, 2, -3, 3, 4)


def ring_pairs(shift):
    n = len(RING)
    return [(RING[i], RING[(i + shift) % n]) for i in range(n)]


def ring_shift(x, shift):
    return lax.ppermute(x, "dp", ring_pairs(shift))


def swap(x, bits):
    return lax.ppermute(x, "tensor", [(i, i ^ bits) for i in range(4)])


CORE, CHIP = 1, 2


def vmem():
    return pl.BlockSpec(memory_space=pltpu.VMEM)


def smem():
    return pl.BlockSpec(memory_space=pltpu.SMEM)


def dot(a, b, ca, cb):
    return lax.dot_general(a, b, (((ca,), (cb,)), ((), ())), preferred_element_type=F32)


def head_mask(h, axis):
    return lax.broadcasted_iota(jnp.int32, (BLOCK, BLOCK), axis) // HD == h


def attn_fwd_kernel(t_ref, qkv_ref, mixed_ref, mixed_t_ref, lse_ref):
    t = t_ref[0]
    heads = BLOCK // HD
    zero = jnp.zeros((BLOCK, BLOCK), BF)
    for i in range(4):
        ri = i ^ t
        q_t = qkv_ref[0, ri].T
        outs = []
        for h in range(heads):
            q_h = jnp.where(head_mask(h, 0), q_t, zero)
            s = [dot(qkv_ref[1, j ^ t], q_h, 1, 0) for j in range(i + 1)]
            top = jnp.max(s[0], axis=0, keepdims=True)
            for sj in s[1:]:
                top = jnp.maximum(top, jnp.max(sj, axis=0, keepdims=True))
            e = [jnp.exp2((sj - top) * (SCORE_SCALE * LOG2E)) for sj in s]
            total = sum(jnp.sum(ej, axis=0, keepdims=True) for ej in e)
            inv = 1.0 / total
            o = None
            for j in range(i + 1):
                v_t = qkv_ref[2, j ^ t].T[h * HD : (h + 1) * HD]
                part = dot(v_t, (e[j] * inv).astype(BF), 1, 0)
                o = part if o is None else o + part
            outs.append(o)
            lse_ref[ri, h : h + 1, :] = top * (SCORE_SCALE * LOG2E) + jnp.log2(total)
        o_t = jnp.concatenate(outs, axis=0).astype(BF)
        mixed_t_ref[ri] = o_t
        mixed_ref[ri] = o_t.T


def attn_bwd_kernel(t_ref, qkv_ref, mixed_t_ref, lse_ref, dmix_ref, out_ref, dk_ref, dv_ref):
    t = t_ref[0]
    heads = BLOCK // HD
    zero = jnp.zeros((BLOCK, BLOCK), BF)
    for i in range(4):
        ri = i ^ t
        q = qkv_ref[0, ri]
        q_t = q.T
        dm = dmix_ref[ri]
        dm_t = dm.T
        prod = dm_t.astype(F32) * mixed_t_ref[ri].astype(F32)
        dqs = []
        for h in range(heads):
            rows, cols = head_mask(h, 0), head_mask(h, 1)
            q_h, qt_h = jnp.where(cols, q, zero), jnp.where(rows, q_t, zero)
            dm_h, dmt_h = jnp.where(cols, dm, zero), jnp.where(rows, dm_t, zero)
            centre = jnp.sum(prod[h * HD : (h + 1) * HD], axis=0, keepdims=True)
            lse = lse_ref[ri, h : h + 1, :]
            dq = None
            for j in range(i + 1):
                rj = j ^ t
                k = qkv_ref[1, rj]
                s = dot(k, qt_h, 1, 0)
                p = jnp.exp2(s * (SCORE_SCALE * LOG2E) - lse)
                dp = dot(qkv_ref[2, rj], dmt_h, 1, 0)
                ds = (p * (dp - centre) * SCORE_SCALE).astype(BF)
                dv = dot(p.astype(BF), dm_h, 1, 0)
                dk = dot(ds, q_h, 1, 0)
                if i == j and h == 0:
                    dk_ref[j], dv_ref[j] = dk, dv
                else:
                    dk_ref[j] += dk
                    dv_ref[j] += dv
                part = dot(k.T[h * HD : (h + 1) * HD], ds, 1, 0)
                dq = part if dq is None else dq + part
            dqs.append(dq)
        out_ref[0, ri] = jnp.concatenate(dqs, axis=0).T.astype(BF)
    for j in range(4):
        out_ref[1, j ^ t] = dk_ref[j].astype(BF)
        out_ref[2, j ^ t] = dv_ref[j].astype(BF)


def attend_forward(t, qkv):
    return pl.pallas_call(
        attn_fwd_kernel,
        out_shape=(
            jax.ShapeDtypeStruct((4, BLOCK, BLOCK), BF),
            jax.ShapeDtypeStruct((4, BLOCK, BLOCK), BF),
            jax.ShapeDtypeStruct((4, 8, BLOCK), F32),
        ),
        in_specs=[smem(), vmem()],
        out_specs=(vmem(), vmem(), vmem()),
        cost_estimate=pl.CostEstimate(
            flops=80 * 2 * BLOCK**3, bytes_accessed=4 << 20, transcendentals=40 * BLOCK**2
        ),
        name="attn_fwd",
    )(t, qkv)


def attend_backward(t, qkv, mixed_t, lse, dmix):
    return pl.pallas_call(
        attn_bwd_kernel,
        out_shape=jax.ShapeDtypeStruct((3, 4, BLOCK, BLOCK), BF),
        in_specs=[smem(), vmem(), vmem(), vmem(), vmem()],
        out_specs=vmem(),
        scratch_shapes=[pltpu.VMEM((4, BLOCK, BLOCK), F32), pltpu.VMEM((4, BLOCK, BLOCK), F32)],
        cost_estimate=pl.CostEstimate(
            flops=200 * 2 * BLOCK**3, bytes_accessed=8 << 20, transcendentals=40 * BLOCK**2
        ),
        name="attn_bwd",
    )(t, qkv, mixed_t, lse, dmix)


def reorder_kernel(idx_ref, *refs):
    n = len(refs) // 2
    for src, dst in zip(refs[:n], refs[n:]):
        w = src.shape[1] // 8
        for k in range(8):
            start = pl.multiple_of(idx_ref[k] * w, 128)
            dst[:, k * w : (k + 1) * w] = src[:, pl.ds(start, w)]


def restore_kernel(idx_ref, *refs):
    n = len(refs) // 2
    for src, dst in zip(refs[:n], refs[n:]):
        w = src.shape[1] // 8
        for k in range(8):
            start = pl.multiple_of(idx_ref[k] * w, 128)
            dst[:, pl.ds(start, w)] = src[:, k * w : (k + 1) * w]


def moved(kernel, idx, *arrays):
    return pl.pallas_call(
        kernel,
        out_shape=[jax.ShapeDtypeStruct(a.shape, a.dtype) for a in arrays],
        in_specs=[smem()] + [vmem()] * len(arrays),
        out_specs=[vmem()] * len(arrays),
        name=kernel.__name__,
    )(idx, *arrays)


def gather_tokens(own):
    other = swap(own, CHIP)
    return swap(own, CORE), other, swap(other, CORE)


def send_far(far):
    rows = far.shape[0] // 2
    passed = swap(far[rows:].astype(BF), CORE)
    return swap((far[:rows] + passed.astype(F32)).astype(BF), CHIP)


def keep_near(near):
    rows = near.shape[0] // 2
    return near[:rows] + swap(near[rows:].astype(BF), CORE).astype(F32)


def gather_dp(shard, axis):
    if lax.axis_size("dp") != len(RING):
        return lax.all_gather(shard, "dp", axis=axis, tiled=True)
    got = {0: shard}
    right = left = shard
    for hop in (1, 2, 3, 4):
        right = ring_shift(right, 1)
        got[4 if hop == 4 else -hop] = right
        if hop < 4:
            left = ring_shift(left, -1)
            got[hop] = left
    return jnp.concatenate([got[o] for o in OFFS], axis=axis)


def scatter_dp(grad, axis):
    parts = lax.axis_size("dp")
    if parts != len(RING):
        return lax.psum_scatter(grad.astype(BF), "dp", scatter_dimension=axis, tiled=True).astype(F32)
    size = grad.shape[axis] // parts

    def part(off):
        return lax.slice_in_dim(grad, OFFS.index(off) * size, (OFFS.index(off) + 1) * size, axis=axis)

    right = ring_shift(part(4).astype(BF), 1)
    left = ring_shift(part(-3).astype(BF), -1)
    for hop in (3, 2, 1):
        right = ring_shift((right.astype(F32) + part(hop)).astype(BF), 1)
        if hop < 3:
            left = ring_shift((left.astype(F32) + part(-hop)).astype(BF), -1)
    return part(0) + right.astype(F32) + left.astype(F32)


def gather_small(gain_attn, gain_ffn, flags):
    if lax.axis_size("dp") != len(RING):
        both = lax.all_gather(jnp.stack([gain_attn, gain_ffn]), ("dp", "tensor"), axis=1, tiled=True)
        return both[0], both[1], lax.psum(jnp.sum(flags), ("dp", "tensor"))
    size = gain_attn.shape[0]
    own = jnp.concatenate([gain_attn, gain_ffn, jnp.sum(flags)[None], jnp.zeros((127 - 2 * size,), F32)])
    own = own[None]
    near = jnp.concatenate([own] + [swap(own, bits) for bits in (1, 2, 3)], axis=0)
    natural = jnp.arange(4) ^ lax.axis_index("tensor")
    near = jnp.sum(
        jnp.where(natural[:, None, None] == jnp.arange(4)[None, :, None], near[None], 0.0), axis=1
    )
    rows = jnp.stack(
        [near] + [ring_shift(near, -o) for o in OFFS[1:]]
    )
    gains_a = rows[:, :, :size].reshape(-1)
    gains_f = rows[:, :, size : 2 * size].reshape(-1)
    return gains_a, gains_f, jnp.sum(rows[:, :, 2 * size])


def reduce_small(grad_a, grad_f, err):
    if lax.axis_size("dp") != len(RING):
        grads = lax.psum_scatter(
            jnp.stack([grad_a, grad_f]), ("dp", "tensor"), scatter_dimension=1, tiled=True
        )
        return grads[0], grads[1], lax.psum(err, ("dp", "tensor"))
    packed = jnp.stack(
        [grad_a.reshape(8, -1), grad_f.reshape(8, -1), jnp.full((8, grad_a.shape[0] // 8), err)], axis=1
    )
    rows = packed[0]
    for k, o in enumerate(OFFS[1:], 1):
        rows = rows + ring_shift(packed[k], o)
    rows = rows + swap(rows, 1) + swap(rows, 2) + swap(rows, 3)
    size = rows.shape[1] // 4
    mine = lax.dynamic_slice_in_dim(rows, lax.axis_index("tensor") * size, size, axis=1)
    return mine[0], mine[1], rows[2, 0]


def norm_forward(values, gain):
    inverse = lax.rsqrt(jnp.mean(values * values, axis=-1, keepdims=True) + EPSILON)
    unit_rows = values * inverse
    return (unit_rows, inverse, (unit_rows * gain).astype(BF))


def norm_backward(grad_normed, unit_rows, inverse, gain):
    grad_gain = jnp.sum(grad_normed * unit_rows, axis=0)
    grad_unit = grad_normed * gain
    centred = grad_unit - unit_rows * jnp.mean(grad_unit * unit_rows, axis=-1, keepdims=True)
    return (inverse * centred, grad_gain)


def cat(*rows):
    return jnp.concatenate(rows, axis=0)


def local(
    tokens, teacher, cotangent, loss_mask, gain_attn, attn_in, attn_out, gain_ffn, ffn_in, ffn_out
):
    ringed = lax.axis_size("dp") == len(RING)
    all_devices = lax.axis_size("dp") * lax.axis_size("tensor")
    rows, width = tokens.shape
    hidden = ffn_out.shape[0]
    local_width = attn_in.shape[2]
    t = lax.axis_index("tensor").astype(jnp.int32)[None]
    flagged = loss_mask.astype(F32)

    full_gain_a, full_gain_f, count = gather_small(gain_attn, gain_ffn, flagged)
    w_in = gather_dp(jnp.moveaxis(attn_in, 1, 0), 1)
    w_out = gather_dp(attn_out, 1)
    w_gu = gather_dp(jnp.transpose(ffn_in, (1, 2, 0)).reshape(2 * hidden, -1), 1)
    w_down = gather_dp(ffn_out, 1)

    if ringed:
        d = lax.axis_index("dp")
        place = jnp.where(d % 2 == 0, d // 2, 7 - d // 2)
        at = (place + jnp.array(OFFS, jnp.int32)) % 8
        idx = jnp.where(at < 4, 2 * at, 2 * (7 - at) + 1).astype(jnp.int32)
        tokens, teacher, cotangent = moved(reorder_kernel, idx, tokens, teacher, cotangent)

    inputs = tokens.astype(F32)
    unit_a, inverse_a, normed_a = norm_forward(inputs, full_gain_a)
    core, chip, both = gather_tokens(normed_a)
    normed_a_full = cat(normed_a, core, chip, both)
    near, far = normed_a_full[: 2 * rows], normed_a_full[2 * rows :]

    def project(rows_in):
        return jnp.einsum("td,cdh->cth", rows_in, w_in, preferred_element_type=F32).astype(BF)

    qkv = jnp.concatenate([project(near), project(far)], axis=1).reshape(3, 4, rows, local_width)
    mixed, mixed_t, lse = attend_forward(t, qkv)
    mixed = mixed.reshape(4 * rows, local_width)
    arrived = send_far(dot(mixed[2 * rows :], w_out, 1, 0))
    hidden_in = inputs + keep_near(dot(mixed[: 2 * rows], w_out, 1, 0)) + arrived.astype(F32)
    unit_f, inverse_f, normed_f = norm_forward(hidden_in, full_gain_f)

    core, chip, both = gather_tokens(normed_f)
    near, far = cat(normed_f, core), cat(chip, both)

    def feed(rows_in):
        gate = dot(rows_in, w_gu[:hidden], 1, 1)
        up = dot(rows_in, w_gu[hidden:], 1, 1)
        inner = (jax.nn.silu(gate) * up).astype(BF)
        return gate, up, inner, dot(inner, w_down, 1, 0)

    fed_near, fed_far = feed(near), feed(far)
    arrived = send_far(fed_far[3])
    result = hidden_in + keep_near(fed_near[3]) + arrived.astype(F32)
    output = result.astype(BF)
    differ = result - teacher.astype(F32)
    err = jnp.sum(flagged[:, None] * differ * differ)
    loss_weight = rows * all_devices / count
    grad_out = cotangent.astype(F32) + 2.0 * loss_weight * flagged[:, None] * differ

    grad_res = grad_out.astype(BF)
    core, chip, both = gather_tokens(grad_res)
    res_near, res_far = cat(grad_res, core), cat(chip, both)

    def feed_back(grads_in, fed):
        gate, up = fed[0], fed[1]
        grad_inner = dot(grads_in, w_down, 1, 1)
        sig = jax.nn.sigmoid(gate)
        grad_gate = grad_inner * up * sig * (1.0 + gate * (1.0 - sig))
        grad_up = grad_inner * (gate * sig)
        grad_gu = jnp.concatenate([grad_gate, grad_up], axis=1).astype(BF)
        return grad_gu, dot(grad_gu, w_gu, 1, 0)

    gu_near, back_near = feed_back(res_near, fed_near)
    gu_far, back_far = feed_back(res_far, fed_far)
    arrived = send_far(back_far)
    grad_normed_f = keep_near(back_near) + arrived.astype(F32)

    grad_ffn_out = scatter_dp(dot(cat(fed_near[2], fed_far[2]), cat(res_near, res_far), 0, 0), 1)
    grad_ffn_in = scatter_dp(dot(cat(gu_near, gu_far), cat(near, far), 0, 0), 1)

    grad_from_norm, grad_gain_f = norm_backward(grad_normed_f, unit_f, inverse_f, full_gain_f)
    grad_hidden = grad_out + grad_from_norm
    grad_branch = grad_hidden.astype(BF)
    core, chip, both = gather_tokens(grad_branch)
    branch_near, branch_far = cat(grad_branch, core), cat(chip, both)
    branch = cat(branch_near, branch_far)
    grad_mixed = cat(
        dot(branch_near, w_out, 1, 1).astype(BF), dot(branch_far, w_out, 1, 1).astype(BF)
    )
    grad_attn_out = scatter_dp(dot(mixed, branch, 0, 0), 1)
    grad_qkv = attend_backward(
        t, qkv, mixed_t, lse, grad_mixed.reshape(4, rows, local_width)
    ).reshape(3, 4 * rows, local_width)

    def project_back(grads_in):
        return jnp.einsum("cth,cdh->td", grads_in, w_in, preferred_element_type=F32)

    arrived = send_far(project_back(grad_qkv[:, 2 * rows :]))
    grad_attn_in = scatter_dp(
        jnp.einsum("td,cth->cdh", normed_a_full, grad_qkv, preferred_element_type=F32), 1
    )
    grad_normed_a = keep_near(project_back(grad_qkv[:, : 2 * rows])) + arrived.astype(F32)
    grad_from_first, grad_gain_a = norm_backward(grad_normed_a, unit_a, inverse_a, full_gain_a)
    grad_tokens = grad_hidden + grad_from_first
    grad_gain_a, grad_gain_f, error_all = reduce_small(grad_gain_a, grad_gain_f, err)
    loss = error_all / (count * width)
    if ringed:
        output, grad_tokens = moved(restore_kernel, idx, output, grad_tokens)
    return (
        output,
        loss,
        grad_tokens,
        grad_gain_a,
        jnp.moveaxis(grad_attn_in, 0, 1),
        grad_attn_out,
        grad_gain_f,
        jnp.transpose(grad_ffn_in.reshape(2, hidden, -1), (2, 0, 1)),
        grad_ffn_out,
    )


def solution(mesh):
    token_rows = P(("dp", "tensor"), None)
    features = P(("dp", "tensor"))
    into, out_of = P("dp", None, "tensor"), P("tensor", "dp")
    return jax.shard_map(
        local,
        mesh=mesh,
        in_specs=(
            token_rows, token_rows, token_rows, features, features, into, out_of, features, into, out_of
        ),
        out_specs=(token_rows, P(), token_rows, features, into, out_of, features, into, out_of),
        check_vma=False,
    )
```

```python
import jax
import jax.numpy as jnp
from jax import lax
from jax.experimental import pallas as pl
from jax.experimental.pallas import tpu as pltpu
from jax.sharding import PartitionSpec as P

HD = 64
BLOCK = 256
EPSILON = 1e-05
SCORE_SCALE = 0.125
LOG2E = 1.4426950408889634
BF = jnp.bfloat16
F32 = jnp.float32

RING = (0, 2, 4, 6, 7, 5, 3, 1)
OFFS = (0, -1, 1, -2, 2, -3, 3, 4)


def ring_pairs(shift):
    n = len(RING)
    return [(RING[i], RING[(i + shift) % n]) for i in range(n)]


def ring_shift(x, shift):
    return lax.ppermute(x, "dp", ring_pairs(shift))


def swap(x, bits):
    return lax.ppermute(x, "tensor", [(i, i ^ bits) for i in range(4)])


CORE, CHIP = 1, 2


def vmem():
    return pl.BlockSpec(memory_space=pltpu.VMEM)


def smem():
    return pl.BlockSpec(memory_space=pltpu.SMEM)


def after(x, *others):
    return lax.optimization_barrier((x,) + others)[0]


def dot(a, b, ca, cb):
    return lax.dot_general(a, b, (((ca,), (cb,)), ((), ())), preferred_element_type=F32)


def head_mask(h, axis):
    return lax.broadcasted_iota(jnp.int32, (BLOCK, BLOCK), axis) // HD == h


def attn_fwd_kernel(at_ref, qkv_ref, mixed_ref, mixed_t_ref, lse_ref, v_t_ref):
    t = at_ref[0]
    zero = jnp.zeros((BLOCK, BLOCK), BF)
    for j in range(4):
        v_t_ref[j] = qkv_ref[j ^ t, :, 2 * BLOCK : 3 * BLOCK].T
    for i in range(4):
        ri = i ^ t
        q_t = qkv_ref[ri, :, :BLOCK].T
        outs = []
        for h in range(BLOCK // HD):
            q_h = jnp.where(head_mask(h, 0), q_t, zero)
            s = [dot(qkv_ref[j ^ t, :, BLOCK : 2 * BLOCK], q_h, 1, 0) for j in range(i + 1)]
            top = jnp.max(s[0], axis=0, keepdims=True)
            for sj in s[1:]:
                top = jnp.maximum(top, jnp.max(sj, axis=0, keepdims=True))
            e = [jnp.exp2((sj - top) * (SCORE_SCALE * LOG2E)) for sj in s]
            total = sum(jnp.sum(ej, axis=0, keepdims=True) for ej in e)
            inv = 1.0 / total
            o = None
            for j in range(i + 1):
                part = dot(v_t_ref[j, h * HD : (h + 1) * HD], (e[j] * inv).astype(BF), 1, 0)
                o = part if o is None else o + part
            outs.append(o)
            lse_ref[ri, h : h + 1, :] = top * (SCORE_SCALE * LOG2E) + jnp.log2(total)
        o_t = jnp.concatenate(outs, axis=0).astype(BF)
        mixed_t_ref[ri] = o_t
        mixed_ref[ri] = o_t.T


def attn_bwd_kernel(
    at_ref, qkv_ref, mixed_t_ref, lse_ref, dmix_ref, out_ref, dk_ref, dv_ref, k_t_ref
):
    t = at_ref[0]
    zero = jnp.zeros((BLOCK, BLOCK), BF)
    for j in range(4):
        k_t_ref[j] = qkv_ref[j ^ t, :, BLOCK : 2 * BLOCK].T
    for i in range(4):
        ri = i ^ t
        q = qkv_ref[ri, :, :BLOCK]
        q_t = q.T
        dm = dmix_ref[ri]
        dm_t = dm.T
        prod = dm_t.astype(F32) * mixed_t_ref[ri].astype(F32)
        dqs = []
        for h in range(BLOCK // HD):
            rows, cols = head_mask(h, 0), head_mask(h, 1)
            q_h, qt_h = jnp.where(cols, q, zero), jnp.where(rows, q_t, zero)
            dm_h, dmt_h = jnp.where(cols, dm, zero), jnp.where(rows, dm_t, zero)
            centre = jnp.sum(prod[h * HD : (h + 1) * HD], axis=0, keepdims=True)
            lse = lse_ref[ri, h : h + 1, :]
            dq = None
            for j in range(i + 1):
                rj = j ^ t
                s = dot(qkv_ref[rj, :, BLOCK : 2 * BLOCK], qt_h, 1, 0)
                p = jnp.exp2(s * (SCORE_SCALE * LOG2E) - lse)
                dp = dot(qkv_ref[rj, :, 2 * BLOCK : 3 * BLOCK], dmt_h, 1, 0)
                ds = (p * (dp - centre) * SCORE_SCALE).astype(BF)
                dv = dot(p.astype(BF), dm_h, 1, 0)
                dk = dot(ds, q_h, 1, 0)
                if i == j and h == 0:
                    dk_ref[j], dv_ref[j] = dk, dv
                else:
                    dk_ref[j] += dk
                    dv_ref[j] += dv
                part = dot(k_t_ref[j, h * HD : (h + 1) * HD], ds, 1, 0)
                dq = part if dq is None else dq + part
            dqs.append(dq)
        out_ref[ri, :, :BLOCK] = jnp.concatenate(dqs, axis=0).T.astype(BF)
    for j in range(4):
        out_ref[j ^ t, :, BLOCK : 2 * BLOCK] = dk_ref[j].astype(BF)
        out_ref[j ^ t, :, 2 * BLOCK : 3 * BLOCK] = dv_ref[j].astype(BF)


def attend_forward(at, qkv):
    return pl.pallas_call(
        attn_fwd_kernel,
        out_shape=(
            jax.ShapeDtypeStruct((4, BLOCK, BLOCK), BF),
            jax.ShapeDtypeStruct((4, BLOCK, BLOCK), BF),
            jax.ShapeDtypeStruct((4, 8, BLOCK), F32),
        ),
        in_specs=[smem(), vmem()],
        out_specs=(vmem(), vmem(), vmem()),
        scratch_shapes=[pltpu.VMEM((4, BLOCK, BLOCK), BF)],
        cost_estimate=pl.CostEstimate(
            flops=80 * 2 * BLOCK**3, bytes_accessed=4 << 20, transcendentals=40 * BLOCK**2
        ),
        name="attn_fwd",
    )(at, qkv)


def attend_backward(at, qkv, mixed_t, lse, dmix):
    return pl.pallas_call(
        attn_bwd_kernel,
        out_shape=jax.ShapeDtypeStruct((4, BLOCK, 3 * BLOCK), BF),
        in_specs=[smem(), vmem(), vmem(), vmem(), vmem()],
        out_specs=vmem(),
        scratch_shapes=[
            pltpu.VMEM((4, BLOCK, BLOCK), F32),
            pltpu.VMEM((4, BLOCK, BLOCK), F32),
            pltpu.VMEM((4, BLOCK, BLOCK), BF),
        ],
        cost_estimate=pl.CostEstimate(
            flops=200 * 2 * BLOCK**3, bytes_accessed=8 << 20, transcendentals=40 * BLOCK**2
        ),
        name="attn_bwd",
    )(at, qkv, mixed_t, lse, dmix)


def block_of(at_ref, k):
    d = at_ref[1]
    place = jnp.where(d % 2 == 0, d // 2, 7 - d // 2)
    ring = (place + OFFS[k] + 8) % 8
    return jnp.where(ring < 4, 2 * ring, 2 * (7 - ring) + 1)


def features(at_ref, k, ringed):
    if not ringed:
        return pl.ds(k * 128, 128)
    return pl.ds(pl.multiple_of(block_of(at_ref, k) * 128, 128), 128)


def row_of(at_ref, k, ringed):
    return pl.ds(block_of(at_ref, k), 1) if ringed else pl.ds(k, 1)


def reorder_kernel(ringed, at_ref, *refs):
    n = len(refs) // 2
    for src, dst in zip(refs[:n], refs[n:]):
        for k in range(8):
            dst[:, k * 128 : (k + 1) * 128] = src[:, features(at_ref, k, ringed)]


def restore_kernel(ringed, at_ref, *refs):
    n = len(refs) // 2
    for src, dst in zip(refs[:n], refs[n:]):
        for k in range(8):
            dst[:, features(at_ref, k, ringed)] = src[:, k * 128 : (k + 1) * 128]


def first_norm_kernel(ringed, at_ref, small_ref, *refs):
    blocks, (normed_ref, gain_a_ref, gain_f_ref) = refs[:4], refs[4:]
    for k in range(8):
        row = row_of(at_ref, k, ringed)
        gain_a_ref[:, k * 128 : (k + 1) * 128] = small_ref[row, :]
        gain_f_ref[:, k * 128 : (k + 1) * 128] = small_ref[pl.ds(8 + row.start, 1), :]
    rows = blocks[0].shape[0]
    for b, ref in enumerate(blocks):
        x = ref[...].astype(F32)
        inverse = lax.rsqrt(jnp.mean(x * x, axis=1, keepdims=True) + EPSILON)
        for k in range(8):
            cols = slice(k * 128, (k + 1) * 128)
            unit = ref[:, features(at_ref, k, ringed)].astype(F32) * inverse
            normed_ref[b * rows : (b + 1) * rows, cols] = (unit * gain_a_ref[:, cols]).astype(BF)


def last_norm_kernel(
    ringed, at_ref, x_ref, gain_ref, hidden_ref, near_ref, core_ref, chip_ref, out_ref
):
    x = x_ref[...].astype(F32)
    inverse = lax.rsqrt(jnp.mean(x * x, axis=1, keepdims=True) + EPSILON)
    unit = x * inverse
    grad = near_ref[...] + core_ref[...].astype(F32) + chip_ref[...].astype(F32)
    c = grad * gain_ref[...]
    middle = jnp.mean(c * unit, axis=1, keepdims=True)
    total = hidden_ref[...] + inverse * (c - unit * middle)
    for k in range(8):
        out_ref[:, features(at_ref, k, ringed)] = total[:, k * 128 : (k + 1) * 128]


def gain_grads_kernel(ringed, at_ref, w_ref, grad_ref, gain_a_ref, grad_f_ref, err_ref, out_ref):
    width = 3 * BLOCK
    prod = w_ref[:, :width].astype(F32) * grad_ref[...]
    ones = jnp.ones((8, width), F32)
    sums = lax.dot_general(
        ones, prod, (((1,), (1,)), ((), ())), precision=lax.Precision.HIGHEST,
        preferred_element_type=F32,
    )[:1] / gain_a_ref[...]
    for k in range(8):
        cols = slice(k * 128, (k + 1) * 128)
        row = row_of(at_ref, k, ringed)
        out_ref[row, :] = sums[:, cols]
        out_ref[pl.ds(8 + row.start, 1), :] = grad_f_ref[:, cols]
    out_ref[16:24, :] = jnp.broadcast_to(err_ref[...], (8, 128))


def call(kernel, ringed, outs, *arrays):
    return pl.pallas_call(
        lambda *refs: kernel(ringed, *refs),
        out_shape=outs,
        in_specs=[smem()] + [vmem()] * (len(arrays) - 1),
        out_specs=jax.tree.map(lambda _: vmem(), outs),
        name=kernel.__name__,
    )(*arrays)


def like(a):
    return jax.ShapeDtypeStruct(a.shape, a.dtype)


def gather_tokens(own):
    other = swap(own, CHIP)
    return swap(own, CORE), other, swap(other, CORE)


def send_far(far):
    rows = far.shape[0] // 2
    passed = swap(far[rows:].astype(BF), CORE)
    return swap((far[:rows] + passed.astype(F32)).astype(BF), CHIP)


def keep_near(near):
    rows = near.shape[0] // 2
    return near[:rows] + swap(near[rows:].astype(BF), CORE).astype(F32)


def gather_dp(shard, axis, split):
    if lax.axis_size("dp") != len(RING):
        return lax.all_gather(shard, "dp", axis=axis, tiled=True), shard
    got = {0: shard}
    right = left = shard
    for hop in (1, 2, 3):
        right, left = ring_shift(right, 1), ring_shift(left, -1)
        got[-hop], got[hop] = right, left
    half = shard.shape[split] // 2
    got[4] = jnp.concatenate(
        [
            ring_shift(lax.slice_in_dim(right, 0, half, axis=split), 1),
            ring_shift(lax.slice_in_dim(left, half, 2 * half, axis=split), -1),
        ],
        axis=split,
    )
    return jnp.concatenate([got[o] for o in OFFS], axis=axis), right


def scatter_dp(grad, axis, split):
    parts = lax.axis_size("dp")
    if parts != len(RING):
        return lax.psum_scatter(grad.astype(BF), "dp", scatter_dimension=axis, tiled=True).astype(F32)
    size = grad.shape[axis] // parts

    def part(off):
        at = OFFS.index(off) * size
        return lax.slice_in_dim(grad, at, at + size, axis=axis)

    def cut(x, second):
        half = x.shape[split] // 2
        return lax.slice_in_dim(x, half * second, half * (second + 1), axis=split)

    right = ring_shift(cut(part(4), 0).astype(BF), 1).astype(F32)
    left = ring_shift(cut(part(4), 1).astype(BF), -1).astype(F32)
    right = jnp.concatenate([cut(part(3), 0) + right, cut(part(3), 1)], axis=split)
    left = jnp.concatenate([cut(part(-3), 0), cut(part(-3), 1) + left], axis=split)
    for hop in (2, 1, 0):
        right = ring_shift(right.astype(BF), 1).astype(F32)
        left = ring_shift(left.astype(BF), -1).astype(F32)
        if hop:
            right, left = right + part(hop), left + part(-hop)
    return part(0) + right + left


def sum_small(x):
    if lax.axis_size("dp") != len(RING):
        return lax.psum(x, ("dp", "tensor"))
    x = x + swap(x, CORE)
    for bits in (1, 2, 4):
        x = x + lax.ppermute(x, "dp", [(i, i ^ bits) for i in range(len(RING))])
    return x + swap(x, CHIP)


def place_small(gain_attn, gain_ffn, flags):
    size = gain_attn.shape[0]
    first = (lax.axis_index("dp") * lax.axis_size("tensor") + lax.axis_index("tensor")) * size
    row = lax.broadcasted_iota(jnp.int32, (24, 128), 0)
    lane = lax.broadcasted_iota(jnp.int32, (24, 128), 1)
    feature = (row % 8) * 128 + lane
    mine = (feature >= first) & (feature < first + size)
    gains = jnp.where(row < 8, jnp.tile(gain_attn, 128 // size)[None], jnp.tile(gain_ffn, 128 // size)[None])
    return jnp.where(row < 16, jnp.where(mine, gains, 0.0), jnp.sum(flags))


def own_features(rows, size):
    first = (lax.axis_index("dp") * lax.axis_size("tensor") + lax.axis_index("tensor")) * size
    return lax.dynamic_slice_in_dim(rows.reshape(-1), first, size)


def norm_forward(values, gain):
    inverse = lax.rsqrt(jnp.mean(values * values, axis=-1, keepdims=True) + EPSILON)
    unit_rows = values * inverse
    return (unit_rows, inverse, (unit_rows * gain).astype(BF))


def norm_backward(grad_normed, unit_rows, inverse, gain):
    grad_gain = jnp.sum(grad_normed * unit_rows, axis=0)
    grad_unit = grad_normed * gain
    centred = grad_unit - unit_rows * jnp.mean(grad_unit * unit_rows, axis=-1, keepdims=True)
    return (inverse * centred, grad_gain)


def cat(*rows):
    return jnp.concatenate(rows, axis=0)


def local(
    tokens, teacher, cotangent, loss_mask, gain_attn, attn_in, attn_out, gain_ffn, ffn_in, ffn_out
):
    ringed = lax.axis_size("dp") == len(RING)
    all_devices = lax.axis_size("dp") * lax.axis_size("tensor")
    rows, width = tokens.shape
    hidden = ffn_out.shape[0]
    inner_width = attn_in.shape[2]
    triple = 3 * inner_width
    at = jnp.stack([lax.axis_index("tensor"), lax.axis_index("dp")]).astype(jnp.int32)
    flagged = loss_mask.astype(F32)

    packed = jnp.concatenate([attn_in[:, 0], attn_in[:, 1], attn_in[:, 2], attn_out.T], axis=1)
    w_attn, third_hop = gather_dp(packed, 0, 1)
    tokens_near = swap(tokens, CORE)
    tokens_chip = swap(tokens, CHIP)
    tokens_both = swap(tokens_chip, CORE)
    small = sum_small(place_small(gain_attn, gain_ffn, flagged))
    packed = cat(jnp.transpose(ffn_in, (1, 2, 0)).reshape(2 * hidden, -1), ffn_out)
    w_ffn, _ = gather_dp(after(packed, third_hop), 1, 0)
    w_gate, w_up, w_down = w_ffn[:hidden], w_ffn[hidden : 2 * hidden], w_ffn[2 * hidden :]

    normed_a, gain_a, gain_f = call(
        first_norm_kernel,
        ringed,
        (
            jax.ShapeDtypeStruct((4 * rows, width), BF),
            jax.ShapeDtypeStruct((1, width), F32),
            jax.ShapeDtypeStruct((1, width), F32),
        ),
        at, small, tokens, tokens_near, tokens_chip, tokens_both,
    )
    count = small[16, 0]
    order = [like(tokens)] * 3
    tokens, teacher, cotangent = call(reorder_kernel, ringed, order, at, tokens, teacher, cotangent)
    inputs = tokens.astype(F32)

    qkv = dot(normed_a, w_attn[:, :triple], 1, 0).astype(BF).reshape(4, rows, triple)
    mixed, mixed_t, lse = attend_forward(at, qkv)
    mixed = mixed.reshape(4 * rows, inner_width)
    w_out = w_attn[:, triple:]
    arrived = send_far(dot(mixed[2 * rows :], w_out, 1, 1))
    hidden_in = inputs + keep_near(dot(mixed[: 2 * rows], w_out, 1, 1)) + arrived.astype(F32)
    unit_f, inverse_f, normed_f = norm_forward(hidden_in, gain_f)

    core, chip, both = gather_tokens(normed_f)
    near, far = cat(normed_f, core), cat(chip, both)

    def feed(rows_in):
        gate = dot(rows_in, w_gate, 1, 1)
        up = dot(rows_in, w_up, 1, 1)
        inner = (jax.nn.silu(gate) * up).astype(BF)
        return gate, up, inner, dot(inner, w_down, 1, 0)

    fed_near, fed_far = feed(near), feed(far)
    arrived = send_far(fed_far[3])
    result = hidden_in + keep_near(fed_near[3]) + arrived.astype(F32)
    differ = result - teacher.astype(F32)
    err = jnp.sum(flagged[:, None] * differ * differ)
    loss_weight = rows * all_devices / count
    grad_out = cotangent.astype(F32) + 2.0 * loss_weight * flagged[:, None] * differ

    grad_res = grad_out.astype(BF)
    core, chip, both = gather_tokens(grad_res)
    res_near, res_far = cat(grad_res, core), cat(chip, both)

    def feed_back(grads_in, fed):
        gate, up = fed[0], fed[1]
        grad_inner = dot(grads_in, w_down, 1, 1)
        sig = jax.nn.sigmoid(gate)
        grad_gate = (grad_inner * up * sig * (1.0 + gate * (1.0 - sig))).astype(BF)
        grad_up = (grad_inner * (gate * sig)).astype(BF)
        return grad_gate, grad_up, dot(grad_gate, w_gate, 1, 0) + dot(grad_up, w_up, 1, 0)

    back_near = feed_back(res_near, fed_near)
    back_far = feed_back(res_far, fed_far)
    arrived = send_far(back_far[2])
    grad_normed_f = keep_near(back_near[2]) + arrived.astype(F32)

    normed_f_full = cat(near, far)
    grad_ffn = scatter_dp(
        cat(
            dot(cat(back_near[0], back_far[0]), normed_f_full, 0, 0),
            dot(cat(back_near[1], back_far[1]), normed_f_full, 0, 0),
            dot(cat(fed_near[2], fed_far[2]), cat(res_near, res_far), 0, 0),
        ),
        1,
        0,
    )

    grad_from_norm, grad_gain_f = norm_backward(grad_normed_f, unit_f, inverse_f, gain_f)
    grad_hidden = grad_out + grad_from_norm
    grad_branch = grad_hidden.astype(BF)
    core, chip, both = gather_tokens(grad_branch)
    branch_near, branch_far = cat(grad_branch, core), cat(chip, both)
    branch = cat(branch_near, branch_far)
    grad_mixed = cat(
        dot(branch_near, w_out, 1, 0).astype(BF), dot(branch_far, w_out, 1, 0).astype(BF)
    )
    grad_attn_out = scatter_dp(dot(branch, mixed, 0, 0), 0, 1)
    grad_qkv = attend_backward(
        at, qkv, mixed_t, lse, grad_mixed.reshape(4, rows, inner_width)
    ).reshape(4 * rows, triple)

    w_in = w_attn[:, :triple]
    arrived = send_far(dot(grad_qkv[2 * rows :], w_in, 1, 1))
    grad_w_in = dot(normed_a, grad_qkv, 0, 0)
    grad_attn_in = scatter_dp(grad_w_in, 0, 1)
    own = dot(grad_qkv[: 2 * rows], w_in, 1, 1)
    passed = swap(own[rows:].astype(BF), CORE)
    small = sum_small(
        call(
            gain_grads_kernel,
            ringed,
            jax.ShapeDtypeStruct((24, 128), F32),
            at, w_attn, grad_w_in, gain_a, grad_gain_f[None], jnp.reshape(err, (1, 1)),
        )
    )
    grad_tokens = call(
        last_norm_kernel,
        ringed,
        jax.ShapeDtypeStruct((rows, width), F32),
        at, tokens, gain_a, grad_hidden, own[:rows], passed, arrived,
    )
    (output,) = call(restore_kernel, ringed, [like(tokens)], at, result.astype(BF))
    loss = small[16, 0] / (count * width)
    size = gain_attn.shape[0]
    return (
        output,
        loss,
        grad_tokens,
        own_features(small[:8], size),
        jnp.stack([grad_attn_in[:, c * inner_width : (c + 1) * inner_width] for c in range(3)], axis=1),
        grad_attn_out.T,
        own_features(small[8:16], size),
        jnp.transpose(grad_ffn[: 2 * hidden].reshape(2, hidden, -1), (2, 0, 1)),
        grad_ffn[2 * hidden :],
    )


def solution(mesh):
    token_rows = P(("dp", "tensor"), None)
    features = P(("dp", "tensor"))
    into, out_of = P("dp", None, "tensor"), P("tensor", "dp")
    return jax.shard_map(
        local,
        mesh=mesh,
        in_specs=(
            token_rows, token_rows, token_rows, features, features, into, out_of, features, into, out_of
        ),
        out_specs=(token_rows, P(), token_rows, features, into, out_of, features, into, out_of),
        check_vma=False,
    )
```

```python
import functools

import jax
import jax.numpy as jnp
from jax import lax
from jax.experimental import pallas as pl
from jax.experimental.pallas import tpu as pltpu
from jax.sharding import PartitionSpec as P


HD = 64
BLOCK = 256
EPSILON = 1e-05
SCORE_SCALE = 0.125
LOG2E = 1.4426950408889634
BF = jnp.bfloat16
F32 = jnp.float32

RING = (0, 2, 4, 6, 7, 5, 3, 1)
OFFS = (0, -1, 1, -2, 2, -3, 3, 4)


def ring_pairs(shift):
    n = len(RING)
    return [(RING[i], RING[(i + shift) % n]) for i in range(n)]


def ring_shift(x, shift):
    return lax.ppermute(x, "dp", ring_pairs(shift))


def swap(x, bits):
    return lax.ppermute(x, "tensor", [(i, i ^ bits) for i in range(4)])


CORE, CHIP = 1, 2


def vmem():
    return pl.BlockSpec(memory_space=pltpu.VMEM)


def smem():
    return pl.BlockSpec(memory_space=pltpu.SMEM)


def after(x, *others):
    return lax.optimization_barrier((x,) + others)[0]


def dot(a, b, ca, cb):
    return lax.dot_general(a, b, (((ca,), (cb,)), ((), ())), preferred_element_type=F32)


def head_mask(h, axis):
    return lax.broadcasted_iota(jnp.int32, (BLOCK, BLOCK), axis) // HD == h


def attn_fwd_kernel(at_ref, qkv_ref, mixed_ref, mixed_t_ref, lse_ref, v_t_ref, o_ref):
    t = at_ref[0]
    zero = jnp.zeros((BLOCK, BLOCK), BF)
    for j in range(4):
        v_t_ref[j] = qkv_ref[j ^ t, :, 2 * BLOCK : 3 * BLOCK].T
    for i in range(4):
        ri = i ^ t
        q_t = qkv_ref[ri, :, :BLOCK].T

        def head(h):
            here = pl.ds(h * HD, HD)
            q_h = jnp.where(head_mask(h, 0), q_t, zero)
            s = [dot(qkv_ref[j ^ t, :, BLOCK : 2 * BLOCK], q_h, 1, 0) for j in range(i + 1)]
            top = jnp.max(s[0], axis=0, keepdims=True)
            for sj in s[1:]:
                top = jnp.maximum(top, jnp.max(sj, axis=0, keepdims=True))
            e = [jnp.exp2((sj - top) * (SCORE_SCALE * LOG2E)) for sj in s]
            total = sum(jnp.sum(ej, axis=0, keepdims=True) for ej in e)
            inv = 1.0 / total
            o = None
            for j in range(i + 1):
                part = dot(v_t_ref[j, here], (e[j] * inv).astype(BF), 1, 0)
                o = part if o is None else o + part
            o_ref[here] = o
            lse_ref[ri, pl.ds(h, 1), :] = top * (SCORE_SCALE * LOG2E) + jnp.log2(total)

        for h in range(BLOCK // HD):
            head(h)
        o_t = o_ref[...].astype(BF)
        mixed_t_ref[ri] = o_t
        mixed_ref[ri] = o_t.T


def attn_bwd_kernel(
    at_ref, qkv_ref, mixed_t_ref, lse_ref, dmix_ref, out_ref,
    dk_ref, dv_ref, k_t_ref, prod_ref, dq_ref,
):
    t = at_ref[0]
    zero = jnp.zeros((BLOCK, BLOCK), BF)
    for j in range(4):
        k_t_ref[j] = qkv_ref[j ^ t, :, BLOCK : 2 * BLOCK].T
    dk_ref[...] = jnp.zeros_like(dk_ref)
    dv_ref[...] = jnp.zeros_like(dv_ref)
    for i in range(4):
        ri = i ^ t
        q = qkv_ref[ri, :, :BLOCK]
        q_t = q.T
        dm = dmix_ref[ri]
        dm_t = dm.T
        prod_ref[...] = dm_t.astype(F32) * mixed_t_ref[ri].astype(F32)

        def head(h):
            here = pl.ds(pl.multiple_of(h * HD, HD), HD)
            rows, cols = head_mask(h, 0), head_mask(h, 1)
            q_h, qt_h = jnp.where(cols, q, zero), jnp.where(rows, q_t, zero)
            dm_h, dmt_h = jnp.where(cols, dm, zero), jnp.where(rows, dm_t, zero)
            centre = jnp.sum(prod_ref[here], axis=0, keepdims=True)
            lse = lse_ref[ri, pl.ds(h, 1), :]
            dq = None
            for j in range(i + 1):
                rj = j ^ t
                s = dot(qkv_ref[rj, :, BLOCK : 2 * BLOCK], qt_h, 1, 0)
                p = jnp.exp2(s * (SCORE_SCALE * LOG2E) - lse)
                dp = dot(qkv_ref[rj, :, 2 * BLOCK : 3 * BLOCK], dmt_h, 1, 0)
                ds = (p * (dp - centre) * SCORE_SCALE).astype(BF)
                dv_ref[j] += dot(p.astype(BF), dm_h, 1, 0)
                dk_ref[j] += dot(ds, q_h, 1, 0)
                part = dot(k_t_ref[j, here], ds, 1, 0)
                dq = part if dq is None else dq + part
            dq_ref[here] = dq

        if i == 0:
            for h in range(BLOCK // HD):
                head(h)
        else:

            @pl.loop(0, BLOCK // HD)
            def _(h):
                head(h)

        out_ref[ri, :, :BLOCK] = dq_ref[...].T.astype(BF)
    for j in range(4):
        out_ref[j ^ t, :, BLOCK : 2 * BLOCK] = dk_ref[j].astype(BF)
        out_ref[j ^ t, :, 2 * BLOCK : 3 * BLOCK] = dv_ref[j].astype(BF)


def room(mib):
    return pltpu.CompilerParams(vmem_limit_bytes=mib << 20)


def attend_forward(at, qkv):
    return pl.pallas_call(
        attn_fwd_kernel,
        out_shape=(
            jax.ShapeDtypeStruct((4, BLOCK, BLOCK), BF),
            jax.ShapeDtypeStruct((4, BLOCK, BLOCK), BF),
            jax.ShapeDtypeStruct((4, 8, BLOCK), F32),
        ),
        in_specs=[smem(), vmem()],
        out_specs=(vmem(), vmem(), vmem()),
        scratch_shapes=[pltpu.VMEM((4, BLOCK, BLOCK), BF), pltpu.VMEM((BLOCK, BLOCK), F32)],
        compiler_params=room(16),
        cost_estimate=pl.CostEstimate(
            flops=80 * 2 * BLOCK**3, bytes_accessed=4 << 20, transcendentals=40 * BLOCK**2
        ),
        name="attn_fwd",
    )(at, qkv)


def attend_backward(at, qkv, mixed_t, lse, dmix):
    return pl.pallas_call(
        attn_bwd_kernel,
        out_shape=jax.ShapeDtypeStruct((4, BLOCK, 3 * BLOCK), BF),
        in_specs=[smem(), vmem(), vmem(), vmem(), vmem()],
        out_specs=vmem(),
        scratch_shapes=[
            pltpu.VMEM((4, BLOCK, BLOCK), F32),
            pltpu.VMEM((4, BLOCK, BLOCK), F32),
            pltpu.VMEM((4, BLOCK, BLOCK), BF),
            pltpu.VMEM((BLOCK, BLOCK), F32),
            pltpu.VMEM((BLOCK, BLOCK), F32),
        ],
        compiler_params=room(20),
        cost_estimate=pl.CostEstimate(
            flops=200 * 2 * BLOCK**3, bytes_accessed=8 << 20, transcendentals=40 * BLOCK**2
        ),
        name="attn_bwd",
    )(at, qkv, mixed_t, lse, dmix)


def block_of(at_ref, k):
    d = at_ref[1]
    place = jnp.where(d % 2 == 0, d // 2, 7 - d // 2)
    ring = (place + OFFS[k] + 8) % 8
    return jnp.where(ring < 4, 2 * ring, 2 * (7 - ring) + 1)


def features(at_ref, k, ringed):
    if not ringed:
        return pl.ds(k * 128, 128)
    return pl.ds(pl.multiple_of(block_of(at_ref, k) * 128, 128), 128)


def row_of(at_ref, k, ringed):
    return pl.ds(block_of(at_ref, k), 1) if ringed else pl.ds(k, 1)


def reorder_kernel(ringed, at_ref, *refs):
    n = len(refs) // 2
    for src, dst in zip(refs[:n], refs[n:]):
        for k in range(8):
            dst[:, k * 128 : (k + 1) * 128] = src[:, features(at_ref, k, ringed)]


def restore_kernel(ringed, at_ref, *refs):
    n = len(refs) // 2
    for src, dst in zip(refs[:n], refs[n:]):
        for k in range(8):
            dst[:, features(at_ref, k, ringed)] = src[:, k * 128 : (k + 1) * 128]


def first_norm_kernel(ringed, at_ref, *refs):
    blocks, smalls, (normed_ref, gain_a_ref, gain_f_ref, count_ref) = refs[:4], refs[4:12], refs[12:]
    for k, small in enumerate(smalls):
        gain_a_ref[:, k * 128 : (k + 1) * 128] = small[0:1, :]
        gain_f_ref[:, k * 128 : (k + 1) * 128] = small[1:2, :]
    count_ref[...] = sum(small[2:3, :] for small in smalls)
    rows = blocks[0].shape[0]
    for b, ref in enumerate(blocks):
        x = ref[...].astype(F32)
        inverse = lax.rsqrt(jnp.mean(x * x, axis=1, keepdims=True) + EPSILON)
        for k in range(8):
            cols = slice(k * 128, (k + 1) * 128)
            unit = ref[:, features(at_ref, k, ringed)].astype(F32) * inverse
            normed_ref[b * rows : (b + 1) * rows, cols] = (unit * gain_a_ref[:, cols]).astype(BF)


def last_norm_kernel(
    ringed, at_ref, x_ref, gain_ref, hidden_ref, near_ref, core_ref, chip_ref, out_ref
):
    x = x_ref[...].astype(F32)
    inverse = lax.rsqrt(jnp.mean(x * x, axis=1, keepdims=True) + EPSILON)
    unit = x * inverse
    grad = near_ref[...] + core_ref[...].astype(F32) + chip_ref[...].astype(F32)
    c = grad * gain_ref[...]
    middle = jnp.mean(c * unit, axis=1, keepdims=True)
    total = hidden_ref[...] + inverse * (c - unit * middle)
    for k in range(8):
        out_ref[:, features(at_ref, k, ringed)] = total[:, k * 128 : (k + 1) * 128]


def gain_grads_kernel(ringed, at_ref, w_ref, grad_ref, gain_a_ref, grad_f_ref, err_ref, out_ref):
    parts, _, size, width = grad_ref.shape
    for k in range(8):
        cols = slice(k * 128, (k + 1) * 128)
        total = jnp.zeros((128, 128), F32)
        for c in range(3):
            if size == 128:
                grad = grad_ref[k, c]
            else:
                each = parts // 8
                grad = grad_ref[k * each : (k + 1) * each, c].reshape(128, width)
            prod = w_ref[cols, c * width : (c + 1) * width].astype(F32) * grad
            for half in range(width // 128):
                total = total + prod[:, half * 128 : (half + 1) * 128]
        row = jnp.sum(total.T, axis=0, keepdims=True) / gain_a_ref[:, cols]
        at = row_of(at_ref, k, ringed)
        out_ref[at, :] = row
        out_ref[pl.ds(8 + at.start, 1), :] = grad_f_ref[:, cols]
    out_ref[16:24, :] = jnp.broadcast_to(err_ref[...], (8, 128))


def attn_wgrad_kernel(ringed, at_ref, normed_ref, grad_ref, out_ref):
    _, _, size, width = out_ref.shape
    for first in range(0, normed_ref.shape[1], 256):
        part = dot(normed_ref[:, first : first + 256], grad_ref[...], 0, 0)
        for r in range(256 // size):
            for c in range(3):
                out_ref[first // size + r, c] = part[
                    r * size : (r + 1) * size, c * width : (c + 1) * width
                ]


def spread_rows_kernel(first, ringed, at_ref, rows_ref, w_ref, *out_refs):
    width = rows_ref.shape[2]
    w = w_ref[:, first : first + width]
    for b in (3, 2, 1, 0):
        out_refs[b][...] = dot(rows_ref[b], w, 1, 1).astype(out_refs[b].dtype)


def call(kernel, ringed, outs, *arrays):
    return pl.pallas_call(
        lambda *refs: kernel(ringed, *refs),
        out_shape=outs,
        in_specs=[smem()] + [vmem()] * (len(arrays) - 1),
        out_specs=jax.tree.map(lambda _: vmem(), outs),
        compiler_params=room(20),
    )(*arrays)


def spread_rows(first, at, blocks, w):
    rows, width = blocks.shape[1], w.shape[0]
    kinds = [jax.ShapeDtypeStruct((rows, width), kind) for kind in (F32, BF, F32, BF)]
    return call(functools.partial(spread_rows_kernel, first), True, kinds, at, blocks, w)


def like(a):
    return jax.ShapeDtypeStruct(a.shape, a.dtype)


def gather_tokens(own):
    other = swap(own, CHIP)
    return swap(own, CORE), other


def send_far(second, third):
    passed = swap(third.astype(BF), CORE)
    return swap((second + passed.astype(F32)).astype(BF), CHIP)


def halves(rows):
    half = rows.shape[0] // 2
    return rows[:half], rows[half:]


def gather_dp(shard, axis, split):
    if lax.axis_size("dp") != len(RING):
        return lax.all_gather(shard, "dp", axis=axis, tiled=True), shard
    got = {0: shard}
    right = left = shard
    for hop in (1, 2, 3):
        right = ring_shift(right, 1)
        left = ring_shift(left, -1)
        got[-hop], got[hop] = right, left
    half = shard.shape[split] // 2
    last = (
        ring_shift(lax.slice_in_dim(right, 0, half, axis=split), 1),
        ring_shift(lax.slice_in_dim(left, half, 2 * half, axis=split), -1),
    )
    got[4] = jnp.concatenate(last, axis=split)
    return jnp.concatenate([got[o] for o in OFFS], axis=axis), right


def scatter_dp(parts, split):
    if lax.axis_size("dp") != len(RING):
        whole = jnp.stack(parts).astype(BF)
        return lax.psum_scatter(whole, "dp", scatter_dimension=0, tiled=True)[0].astype(F32)

    def part(off):
        return parts[OFFS.index(off)]

    def cut(x, second):
        half = x.shape[split] // 2
        return lax.slice_in_dim(x, half * second, half * (second + 1), axis=split)

    right = ring_shift(cut(part(4), 0).astype(BF), 1).astype(F32)
    left = ring_shift(cut(part(4), 1).astype(BF), -1).astype(F32)
    right = jnp.concatenate([cut(part(3), 0) + right, cut(part(3), 1)], axis=split)
    left = jnp.concatenate([cut(part(-3), 0), cut(part(-3), 1) + left], axis=split)
    for hop in (2, 1, 0):
        right, left = lax.optimization_barrier((right.astype(BF), left.astype(BF)))
        right = ring_shift(right, 1).astype(F32)
        left = ring_shift(left, -1).astype(F32)
        if hop:
            right, left = right + part(hop), left + part(-hop)
    return part(0) + right + left


def columns(x):
    size = x.shape[1] // lax.axis_size("dp")
    return [x[:, k * size : (k + 1) * size] for k in range(lax.axis_size("dp"))]


def row_parts(x):
    size = x.shape[0] // lax.axis_size("dp")
    return [x[k * size : (k + 1) * size] for k in range(lax.axis_size("dp"))]


def sum_small(x):
    if lax.axis_size("dp") != len(RING):
        return lax.psum(x, ("dp", "tensor"))
    x = x + swap(x, CORE)
    for bits in (1, 2, 4):
        other = lax.ppermute(x, "dp", [(i, i ^ bits) for i in range(len(RING))])
        x = x + other
    return x + swap(x, CHIP)


def place_kernel(at_ref, gain_a_ref, gain_f_ref, mask_ref, out_ref):
    size = gain_a_ref.shape[1]
    lane = lax.broadcasted_iota(jnp.int32, (1, 128), 1)
    mine = lane // size == at_ref[0]
    for row, ref in enumerate((gain_a_ref, gain_f_ref)):
        tiled = jnp.concatenate([ref[...]] * (128 // size), axis=1)
        out_ref[row : row + 1, :] = jnp.where(mine, tiled, 0.0)
    out_ref[2:8, :] = jnp.broadcast_to(jnp.sum(mask_ref[...].astype(F32)), (6, 128))


def gather_small(at, gain_attn, gain_ffn, mask):
    if lax.axis_size("dp") != len(RING):
        gains = [
            lax.all_gather(g, ("dp", "tensor"), axis=0, tiled=True).reshape(8, 1, 128)
            for g in (gain_attn, gain_ffn)
        ]
        count = lax.psum(jnp.sum(mask.astype(F32)), ("dp", "tensor"))
        rest = jnp.broadcast_to(count / 8, (8, 6, 128))
        return list(jnp.concatenate([*gains, rest], axis=1))
    x = pl.pallas_call(
        place_kernel,
        out_shape=jax.ShapeDtypeStruct((8, 128), F32),
        in_specs=[smem()] + [vmem()] * 3,
        out_specs=vmem(),
        compiler_params=room(2),
        name="place",
    )(at, gain_attn[None], gain_ffn[None], mask.reshape(-1, 128))
    x = x + swap(x, CORE)
    x = x + swap(x, CHIP)
    got = {0: x}
    right = left = x
    for hop in (1, 2, 3):
        right = ring_shift(right, 1)
        left = ring_shift(left, -1)
        got[-hop], got[hop] = right, left
    got[4] = ring_shift(right, 1)
    return [got[o] for o in OFFS]


def own_features(rows, size):
    first = (lax.axis_index("dp") * lax.axis_size("tensor") + lax.axis_index("tensor")) * size
    return lax.dynamic_slice_in_dim(rows.reshape(-1), first, size)


def norm_forward(values, gain):
    inverse = lax.rsqrt(jnp.mean(values * values, axis=-1, keepdims=True) + EPSILON)
    unit_rows = values * inverse
    return (unit_rows, inverse, (unit_rows * gain).astype(BF))


def norm_backward(grad_normed, unit_rows, inverse, gain):
    grad_gain = jnp.sum(grad_normed * unit_rows, axis=0)
    grad_unit = grad_normed * gain
    centred = grad_unit - unit_rows * jnp.mean(grad_unit * unit_rows, axis=-1, keepdims=True)
    return (inverse * centred, grad_gain)


def wgrad(a, b):
    return dot(a, b, 0, 0)


def cat(*rows):
    return jnp.concatenate(rows, axis=0)


def layer(
    tokens, teacher, cotangent, loss_mask, gain_attn, attn_in, attn_out, gain_ffn, ffn_in, ffn_out
):
    parts = lax.axis_size("dp")
    ringed = parts == len(RING)
    all_devices = parts * lax.axis_size("tensor")
    rows, width = tokens.shape
    hidden = ffn_out.shape[0]
    inner_width = attn_in.shape[2]
    triple = 3 * inner_width
    at = jnp.stack([lax.axis_index("tensor"), lax.axis_index("dp")]).astype(jnp.int32)
    flagged = loss_mask.astype(F32)

    packed = jnp.concatenate([attn_in[:, 0], attn_in[:, 1], attn_in[:, 2], attn_out.T], axis=1)
    w_attn, hop = gather_dp(packed, 0, 1)
    tokens_near, tokens_chip = gather_tokens(tokens)
    tokens_both = swap(tokens_chip, CORE)
    smalls = gather_small(at, after(gain_attn, packed), gain_ffn, loss_mask)
    packed = cat(jnp.transpose(ffn_in, (1, 2, 0)).reshape(2 * hidden, -1), ffn_out)
    w_ffn, _ = gather_dp(after(packed, hop), 1, 0)
    w_gate, w_up, w_down = w_ffn[:hidden], w_ffn[hidden : 2 * hidden], w_ffn[2 * hidden :]

    normed_a, gain_a, gain_f, count = call(
        first_norm_kernel,
        ringed,
        (
            jax.ShapeDtypeStruct((4 * rows, width), BF),
            jax.ShapeDtypeStruct((1, width), F32),
            jax.ShapeDtypeStruct((1, width), F32),
            jax.ShapeDtypeStruct((1, 128), F32),
        ),
        at, tokens, tokens_near, tokens_chip, tokens_both, *smalls,
    )
    count = count[0, 0]
    order = [like(tokens)] * 3
    tokens, teacher, cotangent = call(reorder_kernel, ringed, order, at, tokens, teacher, cotangent)
    inputs = tokens.astype(F32)

    qkv = dot(normed_a, w_attn[:, :triple], 1, 0).astype(BF).reshape(4, rows, triple)
    mixed, mixed_t, lse = attend_forward(at, qkv)
    own, partner, far, far_partner = spread_rows(triple, at, mixed, w_attn)
    arrived = send_far(far, far_partner)
    hidden_in = inputs + own + swap(partner, CORE).astype(F32) + arrived.astype(F32)
    unit_f, inverse_f, normed_f = norm_forward(hidden_in, gain_f)

    core, chip = gather_tokens(normed_f)

    def feed(rows_in):
        gate = dot(rows_in, w_gate, 1, 1)
        up = dot(rows_in, w_up, 1, 1)
        inner = (jax.nn.silu(gate) * up).astype(BF)
        return gate, up, inner, dot(inner, w_down, 1, 0)

    near = cat(normed_f, core)
    fed_near = feed(near)
    chip = after(chip, fed_near[3])
    far = cat(chip, swap(chip, CORE))
    fed_far = feed(far)
    own, partner = halves(fed_near[3])
    arrived = send_far(*halves(fed_far[3]))
    result = hidden_in + own + swap(partner.astype(BF), CORE).astype(F32) + arrived.astype(F32)
    differ = result - teacher.astype(F32)
    err = jnp.sum(flagged[:, None] * differ * differ)
    loss_weight = rows * all_devices / count
    grad_out = cotangent.astype(F32) + 2.0 * loss_weight * flagged[:, None] * differ

    grad_res = grad_out.astype(BF)
    core, chip = gather_tokens(grad_res)

    def feed_back(grads_in, fed):
        gate, up = fed[0], fed[1]
        grad_inner = dot(grads_in, w_down, 1, 1)
        sig = jax.nn.sigmoid(gate)
        grad_gate = (grad_inner * up * sig * (1.0 + gate * (1.0 - sig))).astype(BF)
        grad_up = (grad_inner * (gate * sig)).astype(BF)
        return grad_gate, grad_up, dot(grad_gate, w_gate, 1, 0) + dot(grad_up, w_up, 1, 0)

    res_near = cat(grad_res, core)
    back_near = feed_back(res_near, fed_near)
    chip = after(chip, back_near[2])
    res_far = cat(chip, swap(chip, CORE))
    back_far = feed_back(res_far, fed_far)
    own, partner = halves(back_near[2])
    second, third = halves(back_far[2])
    passed = swap(third.astype(BF), CORE)
    sent = (second + passed.astype(F32)).astype(BF)
    arrived = swap(sent, CHIP)
    grad_normed_f = own + swap(partner.astype(BF), CORE).astype(F32) + arrived.astype(F32)

    normed_f_full = after(cat(near, far), sent)
    grad_ffn = scatter_dp(
        columns(
            cat(
                wgrad(cat(back_near[0], back_far[0]), normed_f_full),
                wgrad(cat(back_near[1], back_far[1]), normed_f_full),
                wgrad(cat(fed_near[2], fed_far[2]), after(cat(res_near, res_far), sent)),
            )
        ),
        0,
    )

    grad_from_norm, grad_gain_f = norm_backward(grad_normed_f, unit_f, inverse_f, gain_f)
    grad_hidden = grad_out + grad_from_norm
    grad_branch = grad_hidden.astype(BF)
    core, chip = gather_tokens(grad_branch)
    w_out = w_attn[:, triple:]
    branch_near = cat(grad_branch, core)
    mixed_near = dot(branch_near, w_out, 1, 0).astype(BF)
    chip = after(chip, mixed_near)
    branch_far = cat(chip, swap(chip, CORE))
    grad_mixed = cat(mixed_near, dot(branch_far, w_out, 1, 0).astype(BF))
    grad_qkv = attend_backward(at, qkv, mixed_t, lse, grad_mixed.reshape(4, rows, inner_width))
    own, partner, far, far_partner = spread_rows(0, at, grad_qkv, w_attn)
    passed = swap(far_partner, CORE)
    sent = (far + passed.astype(F32)).astype(BF)
    arrived = swap(sent, CHIP)
    grad_w_in = call(
        attn_wgrad_kernel,
        ringed,
        jax.ShapeDtypeStruct((parts, 3, width // parts, inner_width), F32),
        at, normed_a, after(grad_qkv, far_partner).reshape(4 * rows, triple),
    )
    grad_attn_in = scatter_dp([grad_w_in[k] for k in range(parts)], 2)
    mixed = mixed.reshape(4 * rows, inner_width)
    grad_attn_out = scatter_dp(row_parts(dot(cat(branch_near, branch_far), mixed, 0, 0)), 1)
    passed = swap(partner, CORE)
    small = sum_small(
        call(
            gain_grads_kernel,
            ringed,
            jax.ShapeDtypeStruct((24, 128), F32),
            at, w_attn, after(grad_w_in, sent), gain_a, grad_gain_f[None], jnp.reshape(err, (1, 1)),
        ),
    )
    grad_tokens = call(
        last_norm_kernel,
        ringed,
        jax.ShapeDtypeStruct((rows, width), F32),
        at, tokens, gain_a, grad_hidden, own, passed, arrived,
    )
    (output,) = call(restore_kernel, ringed, [like(tokens)], at, result.astype(BF))
    loss = small[16, 0] / (count * width)
    size = gain_attn.shape[0]
    return (
        output,
        loss,
        grad_tokens,
        own_features(small[:8], size),
        jnp.moveaxis(grad_attn_in, 0, 1),
        grad_attn_out.T,
        own_features(small[8:16], size),
        jnp.transpose(grad_ffn[: 2 * hidden].reshape(2, hidden, -1), (2, 0, 1)),
        grad_ffn[2 * hidden :],
    )


def solution(mesh):
    token_rows = P(("dp", "tensor"), None)
    features = P(("dp", "tensor"))
    into, out_of = P("dp", None, "tensor"), P("tensor", "dp")
    return jax.shard_map(
        layer,
        mesh=mesh,
        in_specs=(
            token_rows, token_rows, token_rows, features, features, into, out_of, features, into, out_of
        ),
        out_specs=(token_rows, P(), token_rows, features, into, out_of, features, into, out_of),
        check_vma=False,
    )
```
